32 devices in a mesh: groups: 2 (over x), tile: 16 (over z, y, core).
Axes of the slice: x: 2, y: 2, z: 4, core: 2. Of those that a mesh axis runs over, the one named last changes fastest.
Arguments:
- tracer_state: float32 [2, 50, 4096], P(None, None, ('groups', 'tile')), parts along dimension 2, may hold values from -6 to 6
- krylov_direction: float32 [2, 50, 4096], P(None, None, ('groups', 'tile')), parts along dimension 2, may hold values from -6 to 6
- explicit_tiles: bfloat16 [800, 6, 128, 128], P('tile')
- implicit_tiles: bfloat16 [800, 3, 128, 128], P('tile')
- explicit_columns: int32 [800, 6], P('tile'), may hold values from 0 to 450, as said below
- ghost_levels: int32 [256, 25], P('tile'), may hold values from 0 to 50, as said below
- wet_levels: int32 [2048], P('tile'), may hold values from 0 to 50
- surface_light: float32 [4096], P(('groups', 'tile')), parts along dimension 0, may hold values from 0.25 to 4
- martin_exponent: float32 [4096], P(('groups', 'tile')), parts along dimension 0, may hold values from 0.5 to 2
- column_slots: int32 [256, 12], P('tile'), may hold values from 0 to 128, as said below
Outputs:
- state_out: float32 [2, 50, 4096], P(None, None, ('groups', 'tile')), parts along dimension 2
- tangent_out: float32 [2, 50, 4096], P(None, None, ('groups', 'tile')), parts along dimension 2
- export_flux: float32 [6144], P(('groups', 'tile')), parts along dimension 0
The draws below stay inside these ranges and needn't reach their ends.
There are 2 independent parts, one for each index of `groups`. The reference program is written for one: setup_inputs(seed, part) draws one part's arguments, and reference() takes and returns one part's arrays. A program takes and returns all parts, laid end to end along the dimension named above; an argument that names none is the same for every part. Nothing has to cross between parts.
Inputs may be any that keep to these rules, and one draw needn't show every extreme that they name: `explicit_columns`: row d * 50 + l holds l, then l - 1 and l + 1 (50 beyond the ends), then one position for each of the devices d - 1, d + 1 and d + D / 2 of the D devices (wrapping), in that order: 51 + s * 25 + l when ghost_levels sends level l from that device s to d, else 50. `ghost_levels`: row s * D + d, slot k, holds k or 50. It holds k exactly for k below a depth of 1 to 25 when s is d - 1, d + 1 or d + D / 2 (wrapping), and 50 for all other pairs; some device gets depth 25 from all three. `column_slots`: row s * D + b lists local columns of device s handed to device b, 128 marking an empty slot. Each column of s with wet_levels above 0 stands exactly once in rows s * D to s * D + D - 1, no dry column does, and some row is full.
All inputs are finite; a program needn't handle non-finite values.
Results may differ from the reference program's by a relative error of at most 0.012.
Values may be sent and summed in bfloat16 or wider, within the bound.
A program may use at most 64 MiB of HBM per device.

```python
import math
import jax
import jax.numpy as jnp
from jax import lax

LEVELS = 50
TRACERS = 2
DEVICE_COLUMNS = 128
NEIGHBOURS = 6
EUPHOTIC = 6
STEPS = 3
GHOST_DEPTH = 25
SLOTS = 12
COLUMNS = 2048
N_TILE = 16


def neighbour_offsets():
    device_count = COLUMNS // DEVICE_COLUMNS
    return jnp.array([1, -1, device_count // 2], dtype=jnp.int32)


def ghost_depths(key):
    device_count = COLUMNS // DEVICE_COLUMNS
    base_key = jax.random.fold_in(key, 11)
    shared_depth = jax.random.randint(base_key, (device_count, 3), 1, GHOST_DEPTH + 1)
    full_receiver = jax.random.randint(jax.random.fold_in(base_key, 1), (), 0, device_count)
    receivers = jnp.arange(device_count, dtype=jnp.int32)[:, None]
    return jnp.where(receivers == full_receiver, GHOST_DEPTH, shared_depth).astype(jnp.int32)


def draw_ghost_levels(key, part):
    device_count = COLUMNS // DEVICE_COLUMNS
    shared_depth = ghost_depths(key)
    receiver = jnp.arange(device_count, dtype=jnp.int32)[None, :, None]
    sender = jnp.arange(device_count, dtype=jnp.int32)[:, None, None]
    matches = (receiver - neighbour_offsets()[None, None, :]) % device_count == sender
    depth_limit = jnp.sum(jnp.where(matches, shared_depth[None, :, :], 0), -1)
    ghost_slot = jnp.arange(GHOST_DEPTH, dtype=jnp.int32)
    levels_sent = jnp.where(ghost_slot[None, None, :] < depth_limit[:, :, None], ghost_slot[None, None, :], LEVELS)
    return levels_sent.reshape(device_count * device_count, GHOST_DEPTH).astype(jnp.int32)


def draw_explicit_columns(key, part):
    device_count = COLUMNS // DEVICE_COLUMNS
    shared_depth = ghost_depths(key)
    level_index = jnp.arange(LEVELS, dtype=jnp.int32)
    index_of_device = jnp.arange(device_count, dtype=jnp.int32)
    own_level = jnp.broadcast_to(level_index[None, :, None], (device_count, LEVELS, 1))
    upper_level = jnp.broadcast_to(jnp.where(level_index >= 1, level_index - 1, LEVELS)[None, :, None], (device_count, LEVELS, 1))
    lower_level = jnp.broadcast_to(jnp.where(level_index < LEVELS - 1, level_index + 1, LEVELS)[None, :, None], (device_count, LEVELS, 1))
    source = (index_of_device[:, None] - neighbour_offsets()[None, :]) % device_count
    remote = jnp.where(level_index[None, :, None] < shared_depth[:, None, :], LEVELS + 1 + source[:, None, :] * GHOST_DEPTH + level_index[None, :, None], LEVELS)
    column_table = jnp.concatenate([own_level, upper_level, lower_level, remote], -1)
    return column_table.reshape(device_count * LEVELS, NEIGHBOURS).astype(jnp.int32)


def column_layout(key):
    device_count = COLUMNS // DEVICE_COLUMNS
    total_slot_count = device_count * SLOTS
    base_key = jax.random.fold_in(key, 23)
    dry_column = jax.random.randint(jax.random.fold_in(base_key, 1), (device_count, DEVICE_COLUMNS), 0, 10) < 3
    column_depth = jax.random.randint(jax.random.fold_in(base_key, 2), (device_count, DEVICE_COLUMNS), 1, LEVELS + 1)
    selected_source = jax.random.randint(jax.random.fold_in(base_key, 3), (), 0, device_count)
    selected_target = jax.random.randint(jax.random.fold_in(base_key, 4), (), 0, device_count)
    split_keys = jax.random.split(jax.random.fold_in(base_key, 5), device_count)
    rating_values = jax.vmap(lambda one_key: jax.random.permutation(one_key, total_slot_count))(split_keys)
    block_of_slots = jnp.arange(total_slot_count, dtype=jnp.int32) // SLOTS
    index_of_device = jnp.arange(device_count, dtype=jnp.int32)
    extra_credit = jnp.where((index_of_device[:, None] == selected_source) & (block_of_slots[None, :] == selected_target), total_slot_count, 0)
    ordering_of_slots = jnp.argsort(-(rating_values + extra_credit), axis=1, stable=True)[:, :DEVICE_COLUMNS]
    forced = (index_of_device[:, None] == selected_source) & (jnp.arange(DEVICE_COLUMNS, dtype=jnp.int32)[None, :] < SLOTS)
    wet_count = jnp.where(dry_column & jnp.logical_not(forced), 0, column_depth)
    column_of_slot = jax.vmap(lambda placed: jnp.full((total_slot_count,), DEVICE_COLUMNS, jnp.int32).at[placed].set(jnp.arange(DEVICE_COLUMNS, dtype=jnp.int32)))(ordering_of_slots)
    clipped = jnp.minimum(column_of_slot, DEVICE_COLUMNS - 1)
    alive_slot = (column_of_slot < DEVICE_COLUMNS) & (jnp.take_along_axis(wet_count, clipped, 1) > 0)
    slot_table = jnp.where(alive_slot, column_of_slot, DEVICE_COLUMNS)
    return (wet_count.reshape(device_count * DEVICE_COLUMNS).astype(jnp.int32), slot_table.reshape(device_count * device_count, SLOTS).astype(jnp.int32))


def draw_wet_levels(key, part):
    return column_layout(key)[0]


def draw_column_slots(key, part):
    return column_layout(key)[1]


def random_tiles(key, tile_shape):
    entries = jax.random.normal(key, tile_shape, jnp.float32)
    return entries


def draw_explicit_tiles(key, part):
    device_count = COLUMNS // DEVICE_COLUMNS
    tile_shape = (device_count * LEVELS, NEIGHBOURS, DEVICE_COLUMNS, DEVICE_COLUMNS)
    entries = random_tiles(jax.random.fold_in(key, 31), tile_shape) * (0.5 / math.sqrt(NEIGHBOURS * DEVICE_COLUMNS))
    entries = entries.at[:, 0].add(0.7 * jnp.eye(DEVICE_COLUMNS, dtype=jnp.float32))
    return entries.astype(jnp.bfloat16)


def draw_implicit_tiles(key, part):
    device_count = COLUMNS // DEVICE_COLUMNS
    tile_shape = (device_count * LEVELS, 3, DEVICE_COLUMNS, DEVICE_COLUMNS)
    entries = random_tiles(jax.random.fold_in(key, 37), tile_shape) * (0.4 / math.sqrt(3 * DEVICE_COLUMNS))
    entries = entries.at[:, 1].add(0.8 * jnp.eye(DEVICE_COLUMNS, dtype=jnp.float32))
    return entries.astype(jnp.bfloat16)


def shard_levels(rng, shape, pieces, low, largest):
    def one(position, blocks):
        steps = jax.random.uniform(jax.random.fold_in(jax.random.fold_in(rng, 6), position), (blocks,), jnp.float32, low / len(pieces), largest / len(pieces))
        return jnp.repeat(jnp.exp(steps), shape[position] // blocks).reshape((-1,) + (1,) * (len(shape) - position - 1))

    gain = one(*pieces[0])
    for cut in pieces[1:]:
        gain = gain * one(*cut)
    return gain


def noise(key, extent, spread, most, cuts=(), kind=jnp.bfloat16):
    values = spread * jax.random.normal(key, extent, jnp.float32)
    if cuts:
        values = values * shard_levels(key, extent, cuts, -0.22, 0.18)
    return jnp.clip(values, -most, most).astype(kind)


def setup_inputs(seed: int = 0, part: int = 0) -> dict:
    key_of = jax.random.split(jax.random.key(seed), 11)
    part_splits = jax.random.split(jax.random.fold_in(key_of[10], part), 11)
    return {
        "tracer_state": noise(part_splits[0], (TRACERS, LEVELS, COLUMNS), 1.0, 6.0, ((2, 16),), jnp.float32),
        "krylov_direction": noise(part_splits[1], (TRACERS, LEVELS, COLUMNS), 1.0, 6.0, ((2, 16),), jnp.float32),
        "explicit_tiles": draw_explicit_tiles(jax.random.fold_in(key_of[10], 71), part),
        "implicit_tiles": draw_implicit_tiles(jax.random.fold_in(key_of[10], 71), part),
        "explicit_columns": draw_explicit_columns(jax.random.fold_in(key_of[10], 71), part),
        "ghost_levels": draw_ghost_levels(jax.random.fold_in(key_of[10], 71), part),
        "wet_levels": draw_wet_levels(jax.random.fold_in(key_of[10], 71), part),
        "surface_light": jnp.clip(jnp.exp(math.log(4.0) - 2.7725887 * jax.random.uniform(part_splits[7], (COLUMNS,), jnp.float32) ** shard_levels(part_splits[7], (COLUMNS,), ((0, 16),), -0.2, 0.2)), 0.25, 4.0),
        "martin_exponent": jnp.clip(jnp.exp(math.log(2.0) - 1.3862944 * jax.random.uniform(part_splits[8], (COLUMNS,), jnp.float32) ** shard_levels(part_splits[8], (COLUMNS,), ((0, 16),), -0.2, 0.2)), 0.5, 2.0),
        "column_slots": draw_column_slots(jax.random.fold_in(key_of[10], 71), part),
    }


max_uptake = 1.0
half_saturation = 0.5
dop_fraction = 0.67
dop_decay = 0.2
time_step = 0.5


def sources(phosphate, organic, depth_count, surface_light, martin_exponent):
    levels = jnp.arange(phosphate.shape[0], dtype=jnp.float32)[:, None]
    wet_mask = (levels < depth_count[None, :]).astype(jnp.float32)
    sunlit = (levels < EUPHOTIC).astype(jnp.float32)
    depth_ratio = (levels + 1.0) ** 1.5 / (EUPHOTIC * 1.0) ** 1.5
    reaching = jnp.where(levels >= EUPHOTIC - 1, jnp.exp(-martin_exponent[None, :] * jnp.log(depth_ratio)), 1.0)
    passing = reaching * (levels < depth_count[None, :] - 1.0).astype(jnp.float32)
    passing_above = jnp.concatenate([jnp.ones_like(passing[:1]), passing[:-1]], 0)
    squared = phosphate * phosphate
    uptake = max_uptake * surface_light[None, :] * jnp.exp(-2.0 * levels / EUPHOTIC) * sunlit * wet_mask * squared / (half_saturation ** 2 + squared)
    export = (1.0 - dop_fraction) * jnp.sum(uptake, 0)
    remineral = export[None, :] * (passing_above - passing)
    decayed = dop_decay * organic * wet_mask
    return -uptake + decayed + remineral, dop_fraction * uptake - decayed, export


def column_sources(columns, params):
    def column_rates(phosphate, organic):
        return sources(phosphate, organic, params[0], params[1], params[2])

    primal, tangent = jax.jvp(column_rates, (columns[:, 0], columns[:, 1]), (columns[:, 2], columns[:, 3]))
    return jnp.stack([primal[0], primal[1], tangent[0], tangent[1]], 1), primal[2]


def explicit_index(explicit_columns, ghost_levels):
    row_count = explicit_columns.shape[0]
    device = (jnp.arange(row_count, dtype=jnp.int32) // LEVELS)[:, None]
    ghost_offset = explicit_columns - LEVELS - 1
    source = jnp.clip(ghost_offset // GHOST_DEPTH, 0, N_TILE - 1).astype(jnp.int32)
    ghost_slot = jnp.clip(ghost_offset % GHOST_DEPTH, 0, GHOST_DEPTH - 1).astype(jnp.int32)
    source_level = ghost_levels[source * N_TILE + device, ghost_slot]
    empty_index = N_TILE * LEVELS
    remote = jnp.where(source_level == LEVELS, empty_index, source * LEVELS + source_level)
    local_index = jnp.where(explicit_columns == LEVELS, empty_index, device * LEVELS + explicit_columns)
    return jnp.where(explicit_columns <= LEVELS, local_index, remote).astype(jnp.int32)


def reference(tracer_state, krylov_direction, explicit_tiles, implicit_tiles, explicit_columns, ghost_levels, wet_levels, surface_light, martin_exponent, column_slots):
    columns = tracer_state.shape[2]
    devices = columns // DEVICE_COLUMNS
    channels = 2 * TRACERS
    depth_count = wet_levels.astype(jnp.float32)
    params = jnp.stack([depth_count, surface_light, martin_exponent])
    wet_mask = (jnp.arange(LEVELS, dtype=jnp.float32)[:, None] < depth_count[None, :]).astype(jnp.float32)
    fields = jnp.concatenate([tracer_state, krylov_direction], 0).transpose(1, 0, 2)
    tile_index = explicit_index(explicit_columns, ghost_levels).reshape(devices, LEVELS, NEIGHBOURS)
    explicit_blocks = explicit_tiles.reshape(devices, LEVELS, NEIGHBOURS, DEVICE_COLUMNS, DEVICE_COLUMNS)
    implicit_blocks = implicit_tiles.reshape(devices, LEVELS, 3, DEVICE_COLUMNS, DEVICE_COLUMNS)

    def to_tiles(values):
        return values.reshape(LEVELS, channels, devices, DEVICE_COLUMNS).transpose(2, 0, 1, 3)

    def from_tiles(values):
        return values.transpose(1, 2, 0, 3).reshape(LEVELS, channels, columns)

    export_total = jnp.zeros((columns,), jnp.float32)
    for time_index in range(STEPS):
        source_rates, export = column_sources(fields, params)
        export_total = export_total + export
        rounded = to_tiles(fields.astype(jnp.bfloat16)).reshape(devices * LEVELS, channels, DEVICE_COLUMNS)
        rounded = jnp.concatenate([rounded, jnp.zeros((1, channels, DEVICE_COLUMNS), jnp.bfloat16)], 0)

        def apply_explicit(operand_pair):
            where_from, blocks = operand_pair
            return jnp.einsum("lkcj,lkji->lci", rounded[where_from].astype(jnp.float32), blocks.astype(jnp.float32))

        carried = lax.map(apply_explicit, (tile_index, explicit_blocks))
        intermediate = (carried + time_step * to_tiles(source_rates)).astype(jnp.bfloat16)
        padded = jnp.pad(intermediate, ((0, 0), (1, 1), (0, 0), (0, 0)))
        stacked = jnp.stack([padded[:, :-2], padded[:, 1:-1], padded[:, 2:]], 2)

        def apply_implicit(operand_pair):
            above_below, blocks = operand_pair
            return jnp.einsum("lkcj,lkji->lci", above_below.astype(jnp.float32), blocks.astype(jnp.float32))

        settled = lax.map(apply_implicit, (stacked, implicit_blocks))
        fields = wet_mask[:, None, :] * from_tiles(settled)
    slot_table = column_slots.reshape(devices, devices, -1).transpose(1, 0, 2)
    source_device = jnp.arange(devices, dtype=jnp.int32)[None, :, None]
    clipped = jnp.minimum(slot_table, DEVICE_COLUMNS - 1).astype(jnp.int32)
    picked = export_total[source_device * DEVICE_COLUMNS + clipped]
    export_flux = jnp.where(slot_table < DEVICE_COLUMNS, picked, 0.0).reshape(-1)
    result = fields.transpose(1, 0, 2)
    return result[:TRACERS], result[TRACERS:], export_flux
```

```python
import jax
import jax.numpy as jnp
from jax import lax
from jax.experimental import pallas as pl
from jax.experimental.pallas import tpu as pltpu
from jax.sharding import PartitionSpec as P

EUPHOTIC = 6
STEPS = 3

max_uptake = 1.0
half_saturation = 0.5
dop_fraction = 0.67
dop_decay = 0.2
time_step = 0.5

MESH = pl.DeviceIdType.MESH
ROWS = 8


def divisor(count, most):
    return max(n for n in range(1, most + 1) if count % n == 0)


def kernel(
    state_ref,
    direction_ref,
    columns_ref,
    wet_ref,
    light_ref,
    martin_ref,
    slots_ref,
    explicit_hbm,
    implicit_hbm,
    state_out,
    tangent_out,
    flux_out,
    local_tiles,
    ghost_tiles,
    implicit_tiles,
    fields,
    middle,
    remineral,
    ghost_mask,
    sending,
    arriving,
    flux_sending,
    flux_arriving,
    local_sem,
    ghost_tile_sem,
    implicit_sem,
    send_sem,
    recv_sem,
    flux_send_sem,
    flux_recv_sem,
):
    tile_count = lax.axis_size("tile")
    me = lax.axis_index("tile")
    tracers, levels, width = state_ref.shape
    slot_count = slots_ref.shape[1]
    chunk = divisor(levels, 10)
    chunks = levels // chunk
    quads = sending.shape[1] // 16
    depth = 3 * width

    def peer_at(offset):
        return lax.rem(me + offset + tile_count, tile_count)

    local_copies = [
        pltpu.make_async_copy(
            explicit_hbm.at[pl.ds(c * chunk, chunk), pl.ds(0, depth), :],
            local_tiles.at[pl.ds(c * chunk, chunk)],
            local_sem.at[c],
        )
        for c in range(chunks)
    ]
    ghost_copy = pltpu.make_async_copy(
        explicit_hbm.at[pl.ds(0, 4 * quads), pl.ds(depth, depth), :],
        ghost_tiles,
        ghost_tile_sem,
    )
    implicit_copies = [
        pltpu.make_async_copy(
            implicit_hbm.at[pl.ds(c * chunk, chunk)],
            implicit_tiles.at[pl.ds(c * chunk, chunk)],
            implicit_sem.at[c],
        )
        for c in range(chunks)
    ]
    for copy in local_copies + [ghost_copy] + implicit_copies:
        copy.start()

    barrier = pltpu.get_barrier_semaphore()
    for offset in range(1, tile_count):
        pl.semaphore_signal(
            barrier, inc=1, device_id={"tile": peer_at(offset)}, device_id_type=MESH
        )

    row = lax.broadcasted_iota(jnp.int32, (ROWS, width), 0)
    upper = row < 4
    depth_count = wet_ref[...].astype(jnp.float32)
    wet_limit = jnp.where(upper, jnp.broadcast_to(depth_count, (ROWS, width)), 0.0)
    light = light_ref[...]
    martin = martin_ref[...]

    zeros = jnp.zeros((ROWS, width), jnp.float32)
    fields[...] = jnp.zeros_like(fields)
    middle[pl.ds(0, ROWS), :] = zeros
    middle[pl.ds((levels + 1) * ROWS, ROWS), :] = zeros
    for c in range(tracers):
        fields[pl.ds(ROWS + c, levels, stride=ROWS), :] = state_ref[c]
        fields[pl.ds(ROWS + tracers + c, levels, stride=ROWS), :] = direction_ref[c]

    level = lax.broadcasted_iota(jnp.int32, (levels, width), 0).astype(jnp.float32)

    def passing(at):
        ratio = jnp.log(jnp.maximum(at + 1.0, 1.0) / EUPHOTIC)
        reaching = jnp.where(at >= EUPHOTIC - 1, jnp.exp(-1.5 * martin * ratio), 1.0)
        kept = jnp.where(at < depth_count - 1.0, reaching, 0.0)
        return jnp.where(at < 0.0, 1.0, kept)

    remineral[...] = time_step * (passing(level - 1.0) - passing(level))

    for k in range(3):
        for l in range(4 * quads):
            shared = (columns_ref[l : l + 1, 3 + k : 4 + k] != levels).astype(jnp.float32)
            ghost_mask[k, pl.ds(4 * l, 4), :] = jnp.broadcast_to(shared, (4, width))
    flux_sending[...] = jnp.zeros_like(flux_sending)

    even = jnp.where((row == 0) | (row == 2), time_step * dop_decay, 0.0)
    odd = jnp.where((row == 1) | (row == 3), time_step * dop_decay, 0.0)
    lit = lax.broadcasted_iota(jnp.int32, (ROWS, width), 0).astype(jnp.float32)
    strength = jnp.where(
        (lit < EUPHOTIC) & (lit < depth_count),
        max_uptake * light * jnp.exp(-2.0 * lit / EUPHOTIC),
        0.0,
    )
    uptake_share = time_step * jnp.where(
        even > 0.0, -1.0, jnp.where(odd > 0.0, dop_fraction, 0.0)
    )

    def at_level(l):
        return pl.ds(pl.multiple_of((l + 1) * ROWS, ROWS), ROWS)

    total = jnp.zeros((1, width), jnp.float32)
    flux_copies = []
    for step in range(STEPS):
        for q in range(quads):
            parts = [fields[at_level(4 * q + j), :] for j in range(4)]
            pairs = [
                jnp.where(upper, parts[2 * h], pltpu.roll(parts[2 * h + 1], 4, 0))
                for h in range(2)
            ]
            sending[step, pl.ds(16 * q, 16), :] = jnp.concatenate(pairs, 0).astype(
                jnp.bfloat16
            )
        if step == 0:
            pl.semaphore_wait(barrier, tile_count - 1)
        copies = []
        for k, offset in enumerate((1, -1, tile_count // 2)):
            copies.append(
                pltpu.make_async_remote_copy(
                    src_ref=sending.at[step],
                    dst_ref=arriving.at[step, k],
                    send_sem=send_sem.at[step, k],
                    recv_sem=recv_sem.at[step, k],
                    device_id={"tile": peer_at(offset)},
                    device_id_type=MESH,
                )
            )
        for copy in copies:
            copy.start()

        phosphate = fields[pl.ds(ROWS, ROWS, stride=ROWS), :]
        direction = fields[pl.ds(ROWS + tracers, ROWS, stride=ROWS), :]
        inverse = 1.0 / (half_saturation**2 + phosphate * phosphate)
        uptake = strength * (phosphate * phosphate) * inverse
        uptake_slope = (
            strength
            * (2.0 * half_saturation**2 * phosphate * inverse)
            * (direction * inverse)
        )
        export = (1.0 - dop_fraction) * jnp.sum(uptake, 0, keepdims=True)
        export_slope = (1.0 - dop_fraction) * jnp.sum(uptake_slope, 0, keepdims=True)
        total = total + export
        sinking = jnp.where(row == 0, export, jnp.where(row == 2, export_slope, 0.0))

        if step == STEPS - 1:
            by_column = jnp.transpose(jnp.broadcast_to(total, (width, width)))
            by_column = by_column[:, :slot_count]
            column = lax.broadcasted_iota(jnp.int32, (width, slot_count), 0)

            def fill(b, carry):
                picked = jnp.where(column == slots_ref[pl.ds(b, 1), :], by_column, 0.0)
                flux_sending[b, 0:1, 0:slot_count] = jnp.sum(picked, 0, keepdims=True)
                return carry

            lax.fori_loop(0, tile_count, fill, 0, unroll=2)
            for offset in range(1, tile_count):
                flux_copies.append(
                    pltpu.make_async_remote_copy(
                        src_ref=flux_sending.at[peer_at(offset)],
                        dst_ref=flux_arriving.at[me],
                        send_sem=flux_send_sem.at[offset],
                        recv_sem=flux_recv_sem.at[offset],
                        device_id={"tile": peer_at(offset)},
                        device_id_type=MESH,
                    )
                )
            for copy in flux_copies:
                copy.start()

        def explicit_chunk(c, carry):
            for i in range(chunk):
                l = c * chunk + i
                here = fields[at_level(l), :]
                above = fields[at_level(l - 1), :]
                below = fields[at_level(l + 1), :]
                source = jnp.concatenate([here, above, below], 1).astype(jnp.bfloat16)
                carried = jnp.dot(
                    source, local_tiles[l], preferred_element_type=jnp.float32
                )
                decay = even * pltpu.roll(here, ROWS - 1, 0) - odd * here
                decay = jnp.where(l.astype(jnp.float32) < wet_limit, decay, 0.0)
                middle[at_level(l), :] = (
                    carried + decay + remineral[pl.ds(l, 1), :] * sinking
                )
            return carry

        def implicit_chunk(c, carry):
            for i in range(chunk):
                l = c * chunk + i
                source = jnp.concatenate(
                    [middle[at_level(l + k - 1), :] for k in range(3)], 1
                ).astype(jnp.bfloat16)
                settled = jnp.dot(
                    source, implicit_tiles[l], preferred_element_type=jnp.float32
                )
                fields[at_level(l), :] = jnp.where(
                    l.astype(jnp.float32) < wet_limit, settled, 0.0
                )
            return carry

        if step == 0:
            for c in range(chunks):
                local_copies[c].wait()
                lax.fori_loop(c, c + 1, explicit_chunk, 0)
        else:
            lax.fori_loop(0, chunks, explicit_chunk, 0)

        for l in range(EUPHOTIC):
            share = jnp.where(
                row < 2, uptake[l : l + 1, :], uptake_slope[l : l + 1, :]
            )
            middle[at_level(l), :] = middle[at_level(l), :] + uptake_share * share

        if step == 0:
            ghost_copy.wait()
        for copy in copies:
            copy.wait_recv()

        def ghost_quad(q, carry):
            rows = pl.ds(pl.multiple_of(16 * q, 16), 16)
            source = jnp.concatenate(
                [
                    arriving[step, k, rows, :].astype(jnp.float32) * ghost_mask[k, rows, :]
                    for k in range(3)
                ],
                1,
            ).astype(jnp.bfloat16)
            for j in range(4):
                l = 4 * q + j
                carried = jnp.dot(
                    source, ghost_tiles[l], preferred_element_type=jnp.float32
                )[8 * (j // 2) : 8 * (j // 2) + 8]
                if j % 2:
                    carried = pltpu.roll(carried, 4, 0)
                middle[at_level(l), :] = middle[at_level(l), :] + jnp.where(
                    upper, carried, 0.0
                )
            return carry

        lax.fori_loop(0, quads, ghost_quad, 0)

        if step == 0:
            for c in range(chunks):
                implicit_copies[c].wait()
                lax.fori_loop(c, c + 1, implicit_chunk, 0)
        else:
            lax.fori_loop(0, chunks, implicit_chunk, 0)
        for copy in copies:
            copy.wait_send()

    for c in range(tracers):
        state_out[c] = fields[pl.ds(ROWS + c, levels, stride=ROWS), :]
        tangent_out[c] = fields[pl.ds(ROWS + tracers + c, levels, stride=ROWS), :]
    for copy in flux_copies:
        copy.wait()
    flux_arriving[me] = flux_sending[me]
    for s in range(tile_count):
        flux_out[s : s + 1, :] = flux_arriving[s, 0:1, 0:slot_count]


def on_device(
    tracer_state,
    krylov_direction,
    explicit_tiles,
    implicit_tiles,
    explicit_columns,
    ghost_levels,
    wet_levels,
    surface_light,
    martin_exponent,
    column_slots,
):
    levels, width = tracer_state.shape[1:]
    tile_count = lax.axis_size("tile")
    slot_count = column_slots.shape[1]
    quads = -(-ghost_levels.shape[1] // 4)
    chunks = levels // divisor(levels, 10)
    vmem = pl.BlockSpec(memory_space=pltpu.VMEM)
    anywhere = pl.BlockSpec(memory_space=pl.ANY)
    state, tangent, flux = pl.pallas_call(
        kernel,
        out_shape=(
            jax.ShapeDtypeStruct(tracer_state.shape, jnp.float32),
            jax.ShapeDtypeStruct(krylov_direction.shape, jnp.float32),
            jax.ShapeDtypeStruct((tile_count, slot_count), jnp.float32),
        ),
        in_specs=[vmem] * 7 + [anywhere] * 2,
        out_specs=(vmem, vmem, vmem),
        scratch_shapes=[
            pltpu.VMEM((levels, 3 * width, width), jnp.bfloat16),
            pltpu.VMEM((4 * quads, 3 * width, width), jnp.bfloat16),
            pltpu.VMEM((levels, 3 * width, width), jnp.bfloat16),
            pltpu.VMEM(((levels + 2) * ROWS, width), jnp.float32),
            pltpu.VMEM(((levels + 2) * ROWS, width), jnp.float32),
            pltpu.VMEM((levels, width), jnp.float32),
            pltpu.VMEM((3, 16 * quads, width), jnp.float32),
            pltpu.VMEM((STEPS, 16 * quads, width), jnp.bfloat16),
            pltpu.VMEM((STEPS, 3, 16 * quads, width), jnp.bfloat16),
            pltpu.VMEM((tile_count, ROWS, width), jnp.float32),
            pltpu.VMEM((tile_count, ROWS, width), jnp.float32),
            pltpu.SemaphoreType.DMA((chunks,)),
            pltpu.SemaphoreType.DMA,
            pltpu.SemaphoreType.DMA((chunks,)),
            pltpu.SemaphoreType.DMA((STEPS, 3)),
            pltpu.SemaphoreType.DMA((STEPS, 3)),
            pltpu.SemaphoreType.DMA((tile_count,)),
            pltpu.SemaphoreType.DMA((tile_count,)),
        ],
        compiler_params=pltpu.CompilerParams(
            collective_id=0, has_side_effects=True, vmem_limit_bytes=40 << 20
        ),
    )(
        tracer_state,
        krylov_direction,
        explicit_columns,
        wet_levels.reshape(1, width),
        surface_light.reshape(1, width),
        martin_exponent.reshape(1, width),
        column_slots,
        explicit_tiles.reshape(levels, -1, width),
        implicit_tiles.reshape(levels, -1, width),
    )
    return (state, tangent, flux.reshape(-1))


def solution(mesh):
    return jax.shard_map(
        on_device,
        mesh=mesh,
        in_specs=(
            P(None, None, ("groups", "tile")),
            P(None, None, ("groups", "tile")),
            P("tile", None, None, None),
            P("tile", None, None, None),
            P("tile", None),
            P("tile", None),
            P("tile"),
            P(("groups", "tile")),
            P(("groups", "tile")),
            P("tile", None),
        ),
        out_specs=(
            P(None, None, ("groups", "tile")),
            P(None, None, ("groups", "tile")),
            P(("groups", "tile")),
        ),
        check_vma=False,
    )
```

```python
import jax
import jax.numpy as jnp
from jax import lax
from jax.experimental import pallas as pl
from jax.experimental.pallas import tpu as pltpu
from jax.sharding import PartitionSpec as P

EUPHOTIC = 6
STEPS = 3

max_uptake = 1.0
half_saturation = 0.5
dop_fraction = 0.67
dop_decay = 0.2
time_step = 0.5

MESH = pl.DeviceIdType.MESH
ROWS = 8


def divisor(count, most):
    return max(n for n in range(1, most + 1) if count % n == 0)


def kernel(
    state_hbm,
    direction_hbm,
    columns_hbm,
    wet_hbm,
    light_hbm,
    martin_hbm,
    slots_hbm,
    explicit_hbm,
    implicit_hbm,
    state_out,
    tangent_out,
    flux_out,
    state_ref,
    direction_ref,
    columns_ref,
    wet_ref,
    light_ref,
    martin_ref,
    slots_ref,
    small_sem,
    local_tiles,
    ghost_tiles,
    implicit_tiles,
    fields,
    middle,
    remineral,
    ghost_mask,
    sending,
    arriving,
    flux_sending,
    flux_arriving,
    local_sem,
    ghost_tile_sem,
    implicit_sem,
    send_sem,
    recv_sem,
    flux_send_sem,
    flux_recv_sem,
):
    tile_count = lax.axis_size("tile")
    me = lax.axis_index("tile")
    levels, tracers, width = state_hbm.shape
    slot_count = slots_ref.shape[1]
    chunk = divisor(levels, 10)
    chunks = levels // chunk
    quads = sending.shape[1] // 16
    depth = 3 * width

    def peer_at(offset):
        return lax.rem(me + offset + tile_count, tile_count)

    local_copies = [
        pltpu.make_async_copy(
            explicit_hbm.at[pl.ds(c * chunk, chunk), pl.ds(0, depth), :],
            local_tiles.at[pl.ds(c * chunk, chunk)],
            local_sem.at[c],
        )
        for c in range(chunks)
    ]
    ghost_copy = pltpu.make_async_copy(
        explicit_hbm.at[pl.ds(0, 4 * quads), pl.ds(depth, depth), :],
        ghost_tiles,
        ghost_tile_sem,
    )
    implicit_copies = [
        pltpu.make_async_copy(
            implicit_hbm.at[pl.ds(c * chunk, chunk)],
            implicit_tiles.at[pl.ds(c * chunk, chunk)],
            implicit_sem.at[c],
        )
        for c in range(chunks)
    ]
    small_copies = [
        pltpu.make_async_copy(source, target, small_sem.at[i])
        for i, (source, target) in enumerate(
            (
                (state_hbm, state_ref),
                (direction_hbm, direction_ref),
                (wet_hbm, wet_ref),
                (light_hbm, light_ref),
                (martin_hbm, martin_ref),
                (columns_hbm, columns_ref),
                (slots_hbm, slots_ref),
            )
        )
    ]
    for copy in small_copies + local_copies + [ghost_copy] + implicit_copies:
        copy.start()

    barrier = pltpu.get_barrier_semaphore()
    for offset in range(1, tile_count):
        pl.semaphore_signal(
            barrier, inc=1, device_id={"tile": peer_at(offset)}, device_id_type=MESH
        )

    fields[...] = jnp.zeros_like(fields)
    flux_sending[...] = jnp.zeros_like(flux_sending)
    for copy in small_copies:
        copy.wait()

    row = lax.broadcasted_iota(jnp.int32, (ROWS, width), 0)
    upper = row < 4
    depth_count = wet_ref[...].astype(jnp.float32)
    wet_limit = jnp.where(upper, jnp.broadcast_to(depth_count, (ROWS, width)), 0.0)
    light = light_ref[...]
    martin = martin_ref[...]

    zeros = jnp.zeros((ROWS, width), jnp.float32)
    middle[pl.ds(0, ROWS), :] = zeros
    middle[pl.ds((levels + 1) * ROWS, ROWS), :] = zeros
    for l in range(levels):
        fields[pl.ds((l + 1) * ROWS, tracers), :] = state_ref[l]
        fields[pl.ds((l + 1) * ROWS + tracers, tracers), :] = direction_ref[l]

    level = lax.broadcasted_iota(jnp.int32, (levels, width), 0).astype(jnp.float32)

    def passing(at):
        ratio = jnp.log(jnp.maximum(at + 1.0, 1.0) / EUPHOTIC)
        reaching = jnp.where(at >= EUPHOTIC - 1, jnp.exp(-1.5 * martin * ratio), 1.0)
        kept = jnp.where(at < depth_count - 1.0, reaching, 0.0)
        return jnp.where(at < 0.0, 1.0, kept)

    remineral[...] = time_step * (passing(level - 1.0) - passing(level))

    for k in range(3):
        for l in range(4 * quads):
            shared = (columns_ref[3 + k : 4 + k, l : l + 1] != levels).astype(jnp.float32)
            ghost_mask[k, pl.ds(4 * l, 4), :] = jnp.broadcast_to(shared, (4, width))

    even = jnp.where((row == 0) | (row == 2), time_step * dop_decay, 0.0)
    odd = jnp.where((row == 1) | (row == 3), time_step * dop_decay, 0.0)
    lit = lax.broadcasted_iota(jnp.int32, (ROWS, width), 0).astype(jnp.float32)
    strength = jnp.where(
        (lit < EUPHOTIC) & (lit < depth_count),
        max_uptake * light * jnp.exp(-2.0 * lit / EUPHOTIC),
        0.0,
    )
    uptake_share = time_step * jnp.where(
        even > 0.0, -1.0, jnp.where(odd > 0.0, dop_fraction, 0.0)
    )

    def at_level(l):
        return pl.ds(pl.multiple_of((l + 1) * ROWS, ROWS), ROWS)

    total = jnp.zeros((1, width), jnp.float32)
    flux_copies = []
    for step in range(STEPS):
        for q in range(quads):
            parts = [fields[at_level(4 * q + j), :] for j in range(4)]
            pairs = [
                jnp.where(upper, parts[2 * h], pltpu.roll(parts[2 * h + 1], 4, 0))
                for h in range(2)
            ]
            sending[step, pl.ds(16 * q, 16), :] = jnp.concatenate(pairs, 0).astype(
                jnp.bfloat16
            )
        if step == 0:
            pl.semaphore_wait(barrier, tile_count - 1)
        copies = []
        for k, offset in enumerate((1, -1, tile_count // 2)):
            copies.append(
                pltpu.make_async_remote_copy(
                    src_ref=sending.at[step],
                    dst_ref=arriving.at[step, k],
                    send_sem=send_sem.at[step, k],
                    recv_sem=recv_sem.at[step, k],
                    device_id={"tile": peer_at(offset)},
                    device_id_type=MESH,
                )
            )
        for copy in copies:
            copy.start()

        phosphate = fields[pl.ds(ROWS, ROWS, stride=ROWS), :]
        direction = fields[pl.ds(ROWS + tracers, ROWS, stride=ROWS), :]
        inverse = 1.0 / (half_saturation**2 + phosphate * phosphate)
        uptake = strength * (phosphate * phosphate) * inverse
        uptake_slope = (
            strength
            * (2.0 * half_saturation**2 * phosphate * inverse)
            * (direction * inverse)
        )
        export = (1.0 - dop_fraction) * jnp.sum(uptake, 0, keepdims=True)
        export_slope = (1.0 - dop_fraction) * jnp.sum(uptake_slope, 0, keepdims=True)
        total = total + export
        sinking = jnp.where(row == 0, export, jnp.where(row == 2, export_slope, 0.0))

        if step == STEPS - 1:
            by_column = jnp.transpose(jnp.broadcast_to(total, (width, width)))
            by_column = by_column[:, :slot_count]
            column = lax.broadcasted_iota(jnp.int32, (width, slot_count), 0)

            def fill(b, carry):
                picked = jnp.where(column == slots_ref[pl.ds(b, 1), :], by_column, 0.0)
                flux_sending[b, 0:1, 0:slot_count] = jnp.sum(picked, 0, keepdims=True)
                return carry

            lax.fori_loop(0, tile_count, fill, 0, unroll=2)
            for offset in range(1, tile_count):
                flux_copies.append(
                    pltpu.make_async_remote_copy(
                        src_ref=flux_sending.at[peer_at(offset)],
                        dst_ref=flux_arriving.at[me],
                        send_sem=flux_send_sem.at[offset],
                        recv_sem=flux_recv_sem.at[offset],
                        device_id={"tile": peer_at(offset)},
                        device_id_type=MESH,
                    )
                )
            for copy in flux_copies:
                copy.start()

        def explicit_chunk(c, carry):
            for i in range(chunk):
                l = c * chunk + i
                here = fields[at_level(l), :]
                above = fields[at_level(l - 1), :]
                below = fields[at_level(l + 1), :]
                source = jnp.concatenate([here, above, below], 1).astype(jnp.bfloat16)
                carried = jnp.dot(
                    source, local_tiles[l], preferred_element_type=jnp.float32
                )
                decay = even * pltpu.roll(here, ROWS - 1, 0) - odd * here
                decay = jnp.where(l.astype(jnp.float32) < wet_limit, decay, 0.0)
                middle[at_level(l), :] = (
                    carried + decay + remineral[pl.ds(l, 1), :] * sinking
                )
            return carry

        def implicit_chunk(c, carry):
            for i in range(chunk):
                l = c * chunk + i
                source = jnp.concatenate(
                    [middle[at_level(l + k - 1), :] for k in range(3)], 1
                ).astype(jnp.bfloat16)
                settled = jnp.dot(
                    source, implicit_tiles[l], preferred_element_type=jnp.float32
                )
                fields[at_level(l), :] = jnp.where(
                    l.astype(jnp.float32) < wet_limit, settled, 0.0
                )
            return carry

        if step == 0:
            for c in range(chunks):
                local_copies[c].wait()
                lax.fori_loop(c, c + 1, explicit_chunk, 0)
        else:
            lax.fori_loop(0, chunks, explicit_chunk, 0)

        for l in range(EUPHOTIC):
            share = jnp.where(
                row < 2, uptake[l : l + 1, :], uptake_slope[l : l + 1, :]
            )
            middle[at_level(l), :] = middle[at_level(l), :] + uptake_share * share

        if step == 0:
            ghost_copy.wait()
        for copy in copies:
            copy.wait_recv()

        def ghost_quad(q, carry):
            rows = pl.ds(pl.multiple_of(16 * q, 16), 16)
            source = jnp.concatenate(
                [
                    arriving[step, k, rows, :].astype(jnp.float32) * ghost_mask[k, rows, :]
                    for k in range(3)
                ],
                1,
            ).astype(jnp.bfloat16)
            for j in range(4):
                l = 4 * q + j
                carried = jnp.dot(
                    source, ghost_tiles[l], preferred_element_type=jnp.float32
                )[8 * (j // 2) : 8 * (j // 2) + 8]
                if j % 2:
                    carried = pltpu.roll(carried, 4, 0)
                middle[at_level(l), :] = middle[at_level(l), :] + jnp.where(
                    upper, carried, 0.0
                )
            return carry

        lax.fori_loop(0, quads, ghost_quad, 0)

        if step == 0:
            for c in range(chunks):
                implicit_copies[c].wait()
                lax.fori_loop(c, c + 1, implicit_chunk, 0)
        else:
            lax.fori_loop(0, chunks, implicit_chunk, 0)
        for copy in copies:
            copy.wait_send()

    for l in range(levels):
        state_out[l] = fields[pl.ds((l + 1) * ROWS, tracers), :]
        tangent_out[l] = fields[pl.ds((l + 1) * ROWS + tracers, tracers), :]
    for copy in flux_copies:
        copy.wait()
    flux_arriving[me] = flux_sending[me]
    for s in range(tile_count):
        flux_out[s : s + 1, :] = flux_arriving[s, 0:1, 0:slot_count]


def on_device(
    tracer_state,
    krylov_direction,
    explicit_tiles,
    implicit_tiles,
    explicit_columns,
    ghost_levels,
    wet_levels,
    surface_light,
    martin_exponent,
    column_slots,
):
    tracers, levels, width = tracer_state.shape
    tile_count = lax.axis_size("tile")
    slot_count = column_slots.shape[1]
    quads = -(-ghost_levels.shape[1] // 4)
    chunks = levels // divisor(levels, 10)
    vmem = pl.BlockSpec(memory_space=pltpu.VMEM)
    anywhere = pl.BlockSpec(memory_space=pl.ANY)
    state, tangent, flux = pl.pallas_call(
        kernel,
        out_shape=(
            jax.ShapeDtypeStruct((levels, tracers, width), jnp.float32),
            jax.ShapeDtypeStruct((levels, tracers, width), jnp.float32),
            jax.ShapeDtypeStruct((tile_count, slot_count), jnp.float32),
        ),
        in_specs=[anywhere] * 9,
        out_specs=(vmem, vmem, vmem),
        scratch_shapes=[
            pltpu.VMEM((levels, tracers, width), jnp.float32),
            pltpu.VMEM((levels, tracers, width), jnp.float32),
            pltpu.VMEM(explicit_columns.shape[::-1], jnp.int32),
            pltpu.VMEM((1, width), jnp.int32),
            pltpu.VMEM((1, width), jnp.float32),
            pltpu.VMEM((1, width), jnp.float32),
            pltpu.VMEM(column_slots.shape, jnp.int32),
            pltpu.SemaphoreType.DMA((7,)),
            pltpu.VMEM((levels, 3 * width, width), jnp.bfloat16),
            pltpu.VMEM((4 * quads, 3 * width, width), jnp.bfloat16),
            pltpu.VMEM((levels, 3 * width, width), jnp.bfloat16),
            pltpu.VMEM(((levels + 2) * ROWS, width), jnp.float32),
            pltpu.VMEM(((levels + 2) * ROWS, width), jnp.float32),
            pltpu.VMEM((levels, width), jnp.float32),
            pltpu.VMEM((3, 16 * quads, width), jnp.float32),
            pltpu.VMEM((STEPS, 16 * quads, width), jnp.bfloat16),
            pltpu.VMEM((STEPS, 3, 16 * quads, width), jnp.bfloat16),
            pltpu.VMEM((tile_count, ROWS, width), jnp.float32),
            pltpu.VMEM((tile_count, ROWS, width), jnp.float32),
            pltpu.SemaphoreType.DMA((chunks,)),
            pltpu.SemaphoreType.DMA,
            pltpu.SemaphoreType.DMA((chunks,)),
            pltpu.SemaphoreType.DMA((STEPS, 3)),
            pltpu.SemaphoreType.DMA((STEPS, 3)),
            pltpu.SemaphoreType.DMA((tile_count,)),
            pltpu.SemaphoreType.DMA((tile_count,)),
        ],
        compiler_params=pltpu.CompilerParams(
            collective_id=0, has_side_effects=True, vmem_limit_bytes=60 << 20
        ),
    )(
        tracer_state.transpose(1, 0, 2),
        krylov_direction.transpose(1, 0, 2),
        explicit_columns.T,
        wet_levels.reshape(1, width),
        surface_light.reshape(1, width),
        martin_exponent.reshape(1, width),
        column_slots,
        explicit_tiles.reshape(levels, -1, width),
        implicit_tiles.reshape(levels, -1, width),
    )
    return (state.transpose(1, 0, 2), tangent.transpose(1, 0, 2), flux.reshape(-1))


def solution(mesh):
    return jax.shard_map(
        on_device,
        mesh=mesh,
        in_specs=(
            P(None, None, ("groups", "tile")),
            P(None, None, ("groups", "tile")),
            P("tile", None, None, None),
            P("tile", None, None, None),
            P("tile", None),
            P("tile", None),
            P("tile"),
            P(("groups", "tile")),
            P(("groups", "tile")),
            P("tile", None),
        ),
        out_specs=(
            P(None, None, ("groups", "tile")),
            P(None, None, ("groups", "tile")),
            P(("groups", "tile")),
        ),
        check_vma=False,
    )
```

```python
import jax
import jax.numpy as jnp
from jax import lax
from jax.experimental import pallas as pl
from jax.experimental.pallas import tpu as pltpu
from jax.sharding import PartitionSpec as P

EUPHOTIC = 6
STEPS = 3

max_uptake = 1.0
half_saturation = 0.5
dop_fraction = 0.67
dop_decay = 0.2
time_step = 0.5

MESH = pl.DeviceIdType.MESH
ROWS = 8


def divisor(count, most):
    return max(n for n in range(1, most + 1) if count % n == 0)


def kernel(
    state_hbm,
    direction_hbm,
    columns_hbm,
    wet_hbm,
    light_hbm,
    martin_hbm,
    slots_hbm,
    explicit_hbm,
    implicit_hbm,
    state_out,
    tangent_out,
    flux_out,
    state_ref,
    direction_ref,
    columns_ref,
    wet_ref,
    light_ref,
    martin_ref,
    slots_ref,
    small_sem,
    local_tiles,
    ghost_tiles,
    implicit_tiles,
    fields,
    middle,
    remineral,
    ghost_mask,
    sending,
    arriving,
    flux_sending,
    flux_arriving,
    local_sem,
    ghost_tile_sem,
    implicit_sem,
    send_sem,
    recv_sem,
    flux_send_sem,
    flux_recv_sem,
):
    tile_count = lax.axis_size("tile")
    me = lax.axis_index("tile")
    levels, tracers, width = state_hbm.shape
    slot_count = slots_ref.shape[1]
    chunk = divisor(levels, 10)
    chunks = levels // chunk
    quads = sending.shape[1] // 16
    depth = 3 * width

    def peer_at(offset):
        return lax.rem(me + offset + tile_count, tile_count)

    local_copies = [
        pltpu.make_async_copy(
            explicit_hbm.at[pl.ds(c * chunk, chunk), pl.ds(0, depth), :],
            local_tiles.at[pl.ds(c * chunk, chunk)],
            local_sem.at[c],
        )
        for c in range(chunks)
    ]
    ghost_copy = pltpu.make_async_copy(
        explicit_hbm.at[pl.ds(0, 4 * quads), pl.ds(depth, depth), :],
        ghost_tiles,
        ghost_tile_sem,
    )
    implicit_copies = [
        pltpu.make_async_copy(
            implicit_hbm.at[pl.ds(c * chunk, chunk)],
            implicit_tiles.at[pl.ds(c * chunk, chunk)],
            implicit_sem.at[c],
        )
        for c in range(chunks)
    ]
    small_copies = [
        pltpu.make_async_copy(source, target, small_sem.at[i])
        for i, (source, target) in enumerate(
            (
                (state_hbm, state_ref),
                (direction_hbm, direction_ref),
                (wet_hbm, wet_ref),
                (light_hbm, light_ref),
                (martin_hbm, martin_ref),
                (columns_hbm, columns_ref),
                (slots_hbm, slots_ref),
            )
        )
    ]
    for copy in small_copies + local_copies + [ghost_copy] + implicit_copies:
        copy.start()

    barrier = pltpu.get_barrier_semaphore()
    for offset in range(1, tile_count):
        pl.semaphore_signal(
            barrier, inc=1, device_id={"tile": peer_at(offset)}, device_id_type=MESH
        )

    fields[...] = jnp.zeros_like(fields)
    flux_sending[...] = jnp.zeros_like(flux_sending)
    for copy in small_copies:
        copy.wait()
    for l in range(levels):
        fields[pl.ds((l + 1) * ROWS, tracers), :] = state_ref[l]
        fields[pl.ds((l + 1) * ROWS + tracers, tracers), :] = direction_ref[l]

    row = lax.broadcasted_iota(jnp.int32, (ROWS, width), 0)
    quad_row = lax.broadcasted_iota(jnp.int32, (2 * ROWS, width), 0) // 4
    upper = row < 4
    pieces = ((0, quads // 2), (quads // 2, quads))
    ghost_copies = [[] for _ in range(STEPS)]

    def at_level(l):
        return pl.ds(pl.multiple_of((l + 1) * ROWS, ROWS), ROWS)

    def pack_piece(step, piece):
        for q in range(*pieces[piece]):
            parts = [fields[at_level(4 * q + j), :] for j in range(4)]
            pairs = [
                jnp.where(upper, parts[2 * h], pltpu.roll(parts[2 * h + 1], 4, 0))
                for h in range(2)
            ]
            sending[step, pl.ds(16 * q, 16), :] = jnp.concatenate(pairs, 0).astype(
                jnp.bfloat16
            )

    def start_piece(step, piece):
        first, last = pieces[piece]
        rows = pl.ds(16 * first, 16 * (last - first))
        copies = [
            pltpu.make_async_remote_copy(
                src_ref=sending.at[step, rows],
                dst_ref=arriving.at[step, k, rows],
                send_sem=send_sem.at[step, piece, k],
                recv_sem=recv_sem.at[step, piece, k],
                device_id={"tile": peer_at(offset)},
                device_id_type=MESH,
            )
            for k, offset in ((2, tile_count // 2), (0, 1), (1, -1))
        ]
        for copy in copies:
            copy.start()
        ghost_copies[step].append(copies)

    def send_piece(step, piece):
        pack_piece(step, piece)
        start_piece(step, piece)

    for piece in range(2):
        pack_piece(0, piece)
    pl.semaphore_wait(barrier, tile_count - 1)
    for piece in range(2):
        start_piece(0, piece)

    depth_count = wet_ref[...].astype(jnp.float32)
    wet_limit = jnp.where(upper, jnp.broadcast_to(depth_count, (ROWS, width)), 0.0)
    light = light_ref[...]
    martin = martin_ref[...]

    zeros = jnp.zeros((ROWS, width), jnp.float32)
    middle[pl.ds(0, ROWS), :] = zeros
    middle[pl.ds((levels + 1) * ROWS, ROWS), :] = zeros

    level = lax.broadcasted_iota(jnp.int32, (levels, width), 0).astype(jnp.float32)

    def passing(at):
        ratio = jnp.log(jnp.maximum(at + 1.0, 1.0) / EUPHOTIC)
        reaching = jnp.where(at >= EUPHOTIC - 1, jnp.exp(-1.5 * martin * ratio), 1.0)
        kept = jnp.where(at < depth_count - 1.0, reaching, 0.0)
        return jnp.where(at < 0.0, 1.0, kept)

    remineral[...] = time_step * (passing(level - 1.0) - passing(level))

    for k in range(3):
        for l in range(4 * quads):
            shared = (columns_ref[3 + k : 4 + k, l : l + 1] != levels).astype(jnp.float32)
            ghost_mask[k, pl.ds(4 * l, 4), :] = jnp.broadcast_to(shared, (4, width))

    even = jnp.where((row == 0) | (row == 2), time_step * dop_decay, 0.0)
    odd = jnp.where((row == 1) | (row == 3), time_step * dop_decay, 0.0)
    lit = lax.broadcasted_iota(jnp.int32, (ROWS, width), 0).astype(jnp.float32)
    strength = jnp.where(
        (lit < EUPHOTIC) & (lit < depth_count),
        max_uptake * light * jnp.exp(-2.0 * lit / EUPHOTIC),
        0.0,
    )
    uptake_share = time_step * jnp.where(
        even > 0.0, -1.0, jnp.where(odd > 0.0, dop_fraction, 0.0)
    )

    def pair_product(first, second, tiles, l):
        blocks = [jnp.concatenate([part, zeros], 0) for part in first]
        blocks += [jnp.concatenate([zeros, part], 0) for part in second]
        return jnp.dot(
            jnp.concatenate(blocks, 1).astype(jnp.bfloat16),
            tiles[pl.ds(l, 2)].reshape(2 * depth, width),
            preferred_element_type=jnp.float32,
        )

    total = jnp.zeros((1, width), jnp.float32)
    flux_copies = []
    for step in range(STEPS):
        phosphate = fields[pl.ds(ROWS, ROWS, stride=ROWS), :]
        direction = fields[pl.ds(ROWS + tracers, ROWS, stride=ROWS), :]
        inverse = 1.0 / (half_saturation**2 + phosphate * phosphate)
        uptake = strength * (phosphate * phosphate) * inverse
        uptake_slope = (
            strength
            * (2.0 * half_saturation**2 * phosphate * inverse)
            * (direction * inverse)
        )
        export = (1.0 - dop_fraction) * jnp.sum(uptake, 0, keepdims=True)
        export_slope = (1.0 - dop_fraction) * jnp.sum(uptake_slope, 0, keepdims=True)
        total = total + export
        sinking = jnp.where(row == 0, export, jnp.where(row == 2, export_slope, 0.0))

        if step == STEPS - 1:
            by_column = jnp.transpose(jnp.broadcast_to(total, (width, width)))
            by_column = by_column[:, :slot_count]
            column = lax.broadcasted_iota(jnp.int32, (width, slot_count), 0)

            def fill(b, carry):
                picked = jnp.where(column == slots_ref[pl.ds(b, 1), :], by_column, 0.0)
                flux_sending[b, 0:1, 0:slot_count] = jnp.sum(picked, 0, keepdims=True)
                return carry

            lax.fori_loop(0, tile_count, fill, 0, unroll=2)
            for offset in range(1, tile_count):
                flux_copies.append(
                    pltpu.make_async_remote_copy(
                        src_ref=flux_sending.at[peer_at(offset)],
                        dst_ref=flux_arriving.at[me],
                        send_sem=flux_send_sem.at[offset],
                        recv_sem=flux_recv_sem.at[offset],
                        device_id={"tile": peer_at(offset)},
                        device_id_type=MESH,
                    )
                )
            for copy in flux_copies:
                copy.start()

        def explicit_chunk(c, carry):
            for i in range(chunk // 2):
                l = c * chunk + 2 * i
                near = [fields[at_level(l + n), :] for n in range(-1, 3)]
                first, second = (near[1], near[0], near[2]), (near[2], near[1], near[3])
                carried = pair_product(first, second, local_tiles, l)
                for n in range(2):
                    here = near[1 + n]
                    decay = even * pltpu.roll(here, ROWS - 1, 0) - odd * here
                    wet = (l + n).astype(jnp.float32) < wet_limit
                    middle[at_level(l + n), :] = (
                        carried[n * ROWS : (n + 1) * ROWS]
                        + jnp.where(wet, decay, 0.0)
                        + remineral[pl.ds(l + n, 1), :] * sinking
                    )
            return carry

        if step == 0:
            for c in range(chunks):
                local_copies[c].wait()
                lax.fori_loop(c, c + 1, explicit_chunk, 0)
        else:
            lax.fori_loop(0, chunks, explicit_chunk, 0)

        for l in range(EUPHOTIC):
            share = jnp.where(
                row < 2, uptake[l : l + 1, :], uptake_slope[l : l + 1, :]
            )
            middle[at_level(l), :] = middle[at_level(l), :] + uptake_share * share

        def ghost_quad(q, carry):
            rows = pl.ds(pl.multiple_of(16 * q, 16), 16)
            sources = [
                arriving[step, k, rows, :].astype(jnp.float32) * ghost_mask[k, rows, :]
                for k in range(3)
            ]
            blocks = [
                jnp.where(quad_row == j, sources[k], 0.0)
                for j in range(4)
                for k in range(3)
            ]
            carried = jnp.dot(
                jnp.concatenate(blocks, 1).astype(jnp.bfloat16),
                ghost_tiles[pl.ds(4 * q, 4)].reshape(4 * depth, width),
                preferred_element_type=jnp.float32,
            )
            for j in range(4):
                part = carried[ROWS * (j // 2) : ROWS * (j // 2) + ROWS]
                if j % 2:
                    part = pltpu.roll(part, 4, 0)
                l = 4 * q + j
                middle[at_level(l), :] = middle[at_level(l), :] + jnp.where(
                    upper, part, 0.0
                )
            return carry

        if step == 0:
            ghost_copy.wait()
        for (first, last), copies in zip(pieces, ghost_copies[step]):
            for copy in copies:
                copy.wait_recv()
            lax.fori_loop(first, last, ghost_quad, 0, unroll=2)

        def implicit_pairs(p, carry):
            l = 2 * p
            near = [middle[at_level(l + n), :] for n in range(-1, 3)]
            settled = pair_product(near[:3], near[1:], implicit_tiles, l)
            for n in range(2):
                wet = (l + n).astype(jnp.float32) < wet_limit
                fields[at_level(l + n), :] = jnp.where(
                    wet, settled[n * ROWS : (n + 1) * ROWS], 0.0
                )
            return carry

        bounds = [4 * last for _, last in pieces] + [levels]
        done, ready = 0, 0
        for i, bound in enumerate(bounds):
            if step == 0:
                while ready * chunk < bound:
                    implicit_copies[ready].wait()
                    ready += 1
            pairs = (bound - done) // 2
            lax.fori_loop(
                done // 2, bound // 2, implicit_pairs, 0, unroll=divisor(pairs, 12)
            )
            done = bound
            if step < STEPS - 1 and i < len(pieces):
                send_piece(step + 1, i)
        for copies in ghost_copies[step]:
            for copy in copies:
                copy.wait_send()

    for l in range(levels):
        state_out[l] = fields[pl.ds((l + 1) * ROWS, tracers), :]
        tangent_out[l] = fields[pl.ds((l + 1) * ROWS + tracers, tracers), :]
    for copy in flux_copies:
        copy.wait()
    flux_arriving[me] = flux_sending[me]
    for s in range(tile_count):
        flux_out[s : s + 1, :] = flux_arriving[s, 0:1, 0:slot_count]


def on_device(
    tracer_state,
    krylov_direction,
    explicit_tiles,
    implicit_tiles,
    explicit_columns,
    ghost_levels,
    wet_levels,
    surface_light,
    martin_exponent,
    column_slots,
):
    tracers, levels, width = tracer_state.shape
    tile_count = lax.axis_size("tile")
    slot_count = column_slots.shape[1]
    quads = -(-ghost_levels.shape[1] // 4)
    chunks = levels // divisor(levels, 10)
    vmem = pl.BlockSpec(memory_space=pltpu.VMEM)
    anywhere = pl.BlockSpec(memory_space=pl.ANY)
    state, tangent, flux = pl.pallas_call(
        kernel,
        out_shape=(
            jax.ShapeDtypeStruct((levels, tracers, width), jnp.float32),
            jax.ShapeDtypeStruct((levels, tracers, width), jnp.float32),
            jax.ShapeDtypeStruct((tile_count, slot_count), jnp.float32),
        ),
        in_specs=[anywhere] * 9,
        out_specs=(vmem, vmem, vmem),
        scratch_shapes=[
            pltpu.VMEM((levels, tracers, width), jnp.float32),
            pltpu.VMEM((levels, tracers, width), jnp.float32),
            pltpu.VMEM(explicit_columns.shape[::-1], jnp.int32),
            pltpu.VMEM((1, width), jnp.int32),
            pltpu.VMEM((1, width), jnp.float32),
            pltpu.VMEM((1, width), jnp.float32),
            pltpu.VMEM(column_slots.shape, jnp.int32),
            pltpu.SemaphoreType.DMA((7,)),
            pltpu.VMEM((levels, 3 * width, width), jnp.bfloat16),
            pltpu.VMEM((4 * quads, 3 * width, width), jnp.bfloat16),
            pltpu.VMEM((levels, 3 * width, width), jnp.bfloat16),
            pltpu.VMEM(((levels + 2) * ROWS, width), jnp.float32),
            pltpu.VMEM(((levels + 2) * ROWS, width), jnp.float32),
            pltpu.VMEM((levels, width), jnp.float32),
            pltpu.VMEM((3, 16 * quads, width), jnp.float32),
            pltpu.VMEM((STEPS, 16 * quads, width), jnp.bfloat16),
            pltpu.VMEM((STEPS, 3, 16 * quads, width), jnp.bfloat16),
            pltpu.VMEM((tile_count, ROWS, width), jnp.float32),
            pltpu.VMEM((tile_count, ROWS, width), jnp.float32),
            pltpu.SemaphoreType.DMA((chunks,)),
            pltpu.SemaphoreType.DMA,
            pltpu.SemaphoreType.DMA((chunks,)),
            pltpu.SemaphoreType.DMA((STEPS, 2, 3)),
            pltpu.SemaphoreType.DMA((STEPS, 2, 3)),
            pltpu.SemaphoreType.DMA((tile_count,)),
            pltpu.SemaphoreType.DMA((tile_count,)),
        ],
        compiler_params=pltpu.CompilerParams(
            collective_id=0, has_side_effects=True, vmem_limit_bytes=60 << 20
        ),
    )(
        tracer_state.transpose(1, 0, 2),
        krylov_direction.transpose(1, 0, 2),
        explicit_columns.T,
        wet_levels.reshape(1, width),
        surface_light.reshape(1, width),
        martin_exponent.reshape(1, width),
        column_slots,
        explicit_tiles.reshape(levels, -1, width),
        implicit_tiles.reshape(levels, -1, width),
    )
    return (state.transpose(1, 0, 2), tangent.transpose(1, 0, 2), flux.reshape(-1))


def solution(mesh):
    return jax.shard_map(
        on_device,
        mesh=mesh,
        in_specs=(
            P(None, None, ("groups", "tile")),
            P(None, None, ("groups", "tile")),
            P("tile", None, None, None),
            P("tile", None, None, None),
            P("tile", None),
            P("tile", None),
            P("tile"),
            P(("groups", "tile")),
            P(("groups", "tile")),
            P("tile", None),
        ),
        out_specs=(
            P(None, None, ("groups", "tile")),
            P(None, None, ("groups", "tile")),
            P(("groups", "tile")),
        ),
        check_vma=False,
    )
```

```python
import jax
import jax.numpy as jnp
from jax import lax
from jax.experimental import pallas as pl
from jax.experimental.pallas import tpu as pltpu
from jax.sharding import PartitionSpec as P

EUPHOTIC = 6
STEPS = 3

max_uptake = 1.0
half_saturation = 0.5
dop_fraction = 0.67
dop_decay = 0.2
time_step = 0.5

MESH = pl.DeviceIdType.MESH
ROWS = 8


def divisor(count, most):
    return max(n for n in range(1, most + 1) if count % n == 0)


def kernel(
    state_hbm,
    direction_hbm,
    columns_hbm,
    wet_hbm,
    light_hbm,
    martin_hbm,
    slots_hbm,
    explicit_hbm,
    implicit_hbm,
    state_out,
    tangent_out,
    flux_out,
    state_ref,
    direction_ref,
    columns_ref,
    wet_ref,
    light_ref,
    martin_ref,
    slots_ref,
    small_sem,
    local_tiles,
    ghost_tiles,
    implicit_tiles,
    fields,
    middle,
    remineral,
    ghost_mask,
    sending,
    arriving,
    flux_sending,
    flux_arriving,
    local_sem,
    ghost_tile_sem,
    implicit_sem,
    send_sem,
    recv_sem,
    flux_send_sem,
    flux_recv_sem,
):
    tile_count = lax.axis_size("tile")
    me = lax.axis_index("tile")
    levels, tracers, width = state_hbm.shape
    slot_count = slots_ref.shape[1]
    chunk = divisor(levels, 10)
    chunks = levels // chunk
    quads = sending.shape[1] // 16
    depth = 3 * width

    def peer_at(offset):
        return lax.rem(me + offset + tile_count, tile_count)

    local_copies = [
        pltpu.make_async_copy(
            explicit_hbm.at[pl.ds(c * chunk, chunk), pl.ds(0, depth), :],
            local_tiles.at[pl.ds(c * chunk, chunk)],
            local_sem.at[c],
        )
        for c in range(chunks)
    ]
    ghost_copy = pltpu.make_async_copy(
        explicit_hbm.at[pl.ds(0, 4 * quads), pl.ds(depth, depth), :],
        ghost_tiles,
        ghost_tile_sem,
    )
    implicit_copies = [
        pltpu.make_async_copy(
            implicit_hbm.at[pl.ds(c * chunk, chunk)],
            implicit_tiles.at[pl.ds(c * chunk, chunk)],
            implicit_sem.at[c],
        )
        for c in range(chunks)
    ]
    small_copies = [
        pltpu.make_async_copy(source, target, small_sem.at[i])
        for i, (source, target) in enumerate(
            (
                (state_hbm, state_ref),
                (direction_hbm, direction_ref),
                (wet_hbm, wet_ref),
                (light_hbm, light_ref),
                (martin_hbm, martin_ref),
                (columns_hbm, columns_ref),
                (slots_hbm, slots_ref),
            )
        )
    ]
    for copy in small_copies + local_copies + [ghost_copy] + implicit_copies:
        copy.start()

    barrier = pltpu.get_barrier_semaphore()
    for offset in range(1, tile_count):
        pl.semaphore_signal(
            barrier, inc=1, device_id={"tile": peer_at(offset)}, device_id_type=MESH
        )

    fields[...] = jnp.zeros_like(fields)
    flux_sending[...] = jnp.zeros_like(flux_sending)
    for copy in small_copies:
        copy.wait()
    for l in range(levels):
        fields[pl.ds((l + 1) * ROWS, tracers), :] = state_ref[l]
        fields[pl.ds((l + 1) * ROWS + tracers, tracers), :] = direction_ref[l]

    row = lax.broadcasted_iota(jnp.int32, (ROWS, width), 0)
    quad_row = lax.broadcasted_iota(jnp.int32, (2 * ROWS, width), 0) // 4
    upper = row < 4
    pieces = ((0, quads // 2), (quads // 2, quads))
    ghost_copies = [[] for _ in range(STEPS)]

    def at_level(l):
        return pl.ds(pl.multiple_of((l + 1) * ROWS, ROWS), ROWS)

    def pack_piece(step, piece):
        for q in range(*pieces[piece]):
            parts = [fields[at_level(4 * q + j), :] for j in range(4)]
            pairs = [
                jnp.where(upper, parts[2 * h], pltpu.roll(parts[2 * h + 1], 4, 0))
                for h in range(2)
            ]
            sending[step, pl.ds(16 * q, 16), :] = jnp.concatenate(pairs, 0).astype(
                jnp.bfloat16
            )

    def start_piece(step, piece):
        first, last = pieces[piece]
        rows = pl.ds(16 * first, 16 * (last - first))
        copies = [
            pltpu.make_async_remote_copy(
                src_ref=sending.at[step, rows],
                dst_ref=arriving.at[step, k, rows],
                send_sem=send_sem.at[step, piece, k],
                recv_sem=recv_sem.at[step, piece, k],
                device_id={"tile": peer_at(offset)},
                device_id_type=MESH,
            )
            for k, offset in ((2, tile_count // 2), (0, 1), (1, -1))
        ]
        for copy in copies:
            copy.start()
        ghost_copies[step].append(copies)

    def send_piece(step, piece):
        pack_piece(step, piece)
        start_piece(step, piece)

    for piece in range(2):
        pack_piece(0, piece)
    pl.semaphore_wait(barrier, tile_count - 1)
    for piece in range(2):
        start_piece(0, piece)

    depth_count = wet_ref[...].astype(jnp.float32)
    wet_limit = jnp.where(upper, jnp.broadcast_to(depth_count, (ROWS, width)), 0.0)
    light = light_ref[...]
    martin = martin_ref[...]

    zeros = jnp.zeros((ROWS, width), jnp.float32)
    middle[pl.ds(0, ROWS), :] = zeros
    middle[pl.ds((levels + 1) * ROWS, ROWS), :] = zeros

    level = lax.broadcasted_iota(jnp.int32, (levels, width), 0).astype(jnp.float32)

    def passing(at):
        ratio = jnp.log(jnp.maximum(at + 1.0, 1.0) / EUPHOTIC)
        reaching = jnp.where(at >= EUPHOTIC - 1, jnp.exp(-1.5 * martin * ratio), 1.0)
        kept = jnp.where(at < depth_count - 1.0, reaching, 0.0)
        return jnp.where(at < 0.0, 1.0, kept)

    remineral[...] = time_step * (passing(level - 1.0) - passing(level))

    for k in range(3):
        for l in range(4 * quads):
            shared = (columns_ref[3 + k : 4 + k, l : l + 1] != levels).astype(jnp.float32)
            ghost_mask[k, pl.ds(4 * l, 4), :] = jnp.broadcast_to(shared, (4, width))

    even = jnp.where((row == 0) | (row == 2), time_step * dop_decay, 0.0)
    odd = jnp.where((row == 1) | (row == 3), time_step * dop_decay, 0.0)
    lit = lax.broadcasted_iota(jnp.int32, (ROWS, width), 0).astype(jnp.float32)
    strength = jnp.where(
        (lit < EUPHOTIC) & (lit < depth_count),
        max_uptake * light * jnp.exp(-2.0 * lit / EUPHOTIC),
        0.0,
    )
    uptake_share = time_step * jnp.where(
        even > 0.0, -1.0, jnp.where(odd > 0.0, dop_fraction, 0.0)
    )

    def pair_product(first, second, tiles, l):
        blocks = [jnp.concatenate([part, zeros], 0) for part in first]
        blocks += [jnp.concatenate([zeros, part], 0) for part in second]
        return jnp.dot(
            jnp.concatenate(blocks, 1).astype(jnp.bfloat16),
            tiles[pl.ds(l, 2)].reshape(2 * depth, width),
            preferred_element_type=jnp.float32,
        )

    total = jnp.zeros((1, width), jnp.float32)
    flux_copies = []
    for step in range(STEPS):
        phosphate = fields[pl.ds(ROWS, ROWS, stride=ROWS), :]
        direction = fields[pl.ds(ROWS + tracers, ROWS, stride=ROWS), :]
        inverse = 1.0 / (half_saturation**2 + phosphate * phosphate)
        uptake = strength * (phosphate * phosphate) * inverse
        uptake_slope = (
            strength
            * (2.0 * half_saturation**2 * phosphate * inverse)
            * (direction * inverse)
        )
        export = (1.0 - dop_fraction) * jnp.sum(uptake, 0, keepdims=True)
        export_slope = (1.0 - dop_fraction) * jnp.sum(uptake_slope, 0, keepdims=True)
        total = total + export
        sinking = jnp.where(row == 0, export, jnp.where(row == 2, export_slope, 0.0))

        if step == STEPS - 1:
            by_column = jnp.transpose(jnp.broadcast_to(total, (width, width)))
            by_column = by_column[:, :slot_count]
            column = lax.broadcasted_iota(jnp.int32, (width, slot_count), 0)

            def fill(b, carry):
                picked = jnp.where(column == slots_ref[pl.ds(b, 1), :], by_column, 0.0)
                flux_sending[b, 0:1, 0:slot_count] = jnp.sum(picked, 0, keepdims=True)
                return carry

            lax.fori_loop(0, tile_count, fill, 0, unroll=2)
            for offset in range(1, tile_count):
                flux_copies.append(
                    pltpu.make_async_remote_copy(
                        src_ref=flux_sending.at[peer_at(offset)],
                        dst_ref=flux_arriving.at[me],
                        send_sem=flux_send_sem.at[offset],
                        recv_sem=flux_recv_sem.at[offset],
                        device_id={"tile": peer_at(offset)},
                        device_id_type=MESH,
                    )
                )
            for copy in flux_copies:
                copy.start()

        def explicit_chunk(c, carry):
            for i in range(chunk // 2):
                l = c * chunk + 2 * i
                near = [fields[at_level(l + n), :] for n in range(-1, 3)]
                first, second = (near[1], near[0], near[2]), (near[2], near[1], near[3])
                carried = pair_product(first, second, local_tiles, l)
                for n in range(2):
                    here = near[1 + n]
                    decay = even * pltpu.roll(here, ROWS - 1, 0) - odd * here
                    wet = (l + n).astype(jnp.float32) < wet_limit
                    middle[at_level(l + n), :] = (
                        carried[n * ROWS : (n + 1) * ROWS]
                        + jnp.where(wet, decay, 0.0)
                        + remineral[pl.ds(l + n, 1), :] * sinking
                    )
            return carry

        if step == 0:
            for c in range(chunks):
                local_copies[c].wait()
                lax.fori_loop(c, c + 1, explicit_chunk, 0)
        else:
            lax.fori_loop(0, chunks, explicit_chunk, 0)

        for l in range(EUPHOTIC):
            share = jnp.where(
                row < 2, uptake[l : l + 1, :], uptake_slope[l : l + 1, :]
            )
            middle[at_level(l), :] = middle[at_level(l), :] + uptake_share * share

        def ghost_quad(q, carry):
            rows = pl.ds(pl.multiple_of(16 * q, 16), 16)
            sources = [
                arriving[step, k, rows, :].astype(jnp.float32) * ghost_mask[k, rows, :]
                for k in range(3)
            ]
            blocks = [
                jnp.where(quad_row == j, sources[k], 0.0)
                for j in range(4)
                for k in range(3)
            ]
            carried = jnp.dot(
                jnp.concatenate(blocks, 1).astype(jnp.bfloat16),
                ghost_tiles[pl.ds(4 * q, 4)].reshape(4 * depth, width),
                preferred_element_type=jnp.float32,
            )
            for j in range(4):
                part = carried[ROWS * (j // 2) : ROWS * (j // 2) + ROWS]
                if j % 2:
                    part = pltpu.roll(part, 4, 0)
                l = 4 * q + j
                middle[at_level(l), :] = middle[at_level(l), :] + jnp.where(
                    upper, part, 0.0
                )
            return carry

        if step == 0:
            ghost_copy.wait()
        for (first, last), copies in zip(pieces, ghost_copies[step]):
            for copy in copies:
                copy.wait_recv()
            lax.fori_loop(first, last, ghost_quad, 0, unroll=2)

        def implicit_pairs(p, carry):
            l = 2 * p
            near = [middle[at_level(l + n), :] for n in range(-1, 3)]
            settled = pair_product(near[:3], near[1:], implicit_tiles, l)
            for n in range(2):
                wet = (l + n).astype(jnp.float32) < wet_limit
                fields[at_level(l + n), :] = jnp.where(
                    wet, settled[n * ROWS : (n + 1) * ROWS], 0.0
                )
            return carry

        bounds = [4 * last for _, last in pieces] + [levels]
        done, ready = 0, 0
        for i, bound in enumerate(bounds):
            if step == 0:
                while ready * chunk < bound:
                    implicit_copies[ready].wait()
                    ready += 1
            pairs = (bound - done) // 2
            lax.fori_loop(
                done // 2, bound // 2, implicit_pairs, 0, unroll=divisor(pairs, 12)
            )
            done = bound
            if step < STEPS - 1 and i < len(pieces):
                send_piece(step + 1, i)
        for copies in ghost_copies[step]:
            for copy in copies:
                copy.wait_send()

    for l in range(levels):
        state_out[l] = fields[pl.ds((l + 1) * ROWS, tracers), :]
        tangent_out[l] = fields[pl.ds((l + 1) * ROWS + tracers, tracers), :]
    for copy in flux_copies:
        copy.wait()
    flux_arriving[me] = flux_sending[me]
    for s in range(tile_count):
        flux_out[s : s + 1, :] = flux_arriving[s, 0:1, 0:slot_count]


def on_device(
    tracer_state,
    krylov_direction,
    explicit_tiles,
    implicit_tiles,
    explicit_columns,
    ghost_levels,
    wet_levels,
    surface_light,
    martin_exponent,
    column_slots,
):
    tracers, levels, width = tracer_state.shape
    tile_count = lax.axis_size("tile")
    slot_count = column_slots.shape[1]
    quads = -(-ghost_levels.shape[1] // 4)
    chunks = levels // divisor(levels, 10)
    vmem = pl.BlockSpec(memory_space=pltpu.VMEM)
    hbm = pl.BlockSpec(memory_space=pltpu.HBM)
    state, tangent, flux = pl.pallas_call(
        kernel,
        out_shape=(
            jax.ShapeDtypeStruct((levels, tracers, width), jnp.float32),
            jax.ShapeDtypeStruct((levels, tracers, width), jnp.float32),
            jax.ShapeDtypeStruct((tile_count, slot_count), jnp.float32),
        ),
        in_specs=[hbm] * 9,
        out_specs=(vmem, vmem, vmem),
        scratch_shapes=[
            pltpu.VMEM((levels, tracers, width), jnp.float32),
            pltpu.VMEM((levels, tracers, width), jnp.float32),
            pltpu.VMEM(explicit_columns.shape[::-1], jnp.int32),
            pltpu.VMEM((1, width), jnp.int32),
            pltpu.VMEM((1, width), jnp.float32),
            pltpu.VMEM((1, width), jnp.float32),
            pltpu.VMEM(column_slots.shape, jnp.int32),
            pltpu.SemaphoreType.DMA((7,)),
            pltpu.VMEM((levels, 3 * width, width), jnp.bfloat16),
            pltpu.VMEM((4 * quads, 3 * width, width), jnp.bfloat16),
            pltpu.VMEM((levels, 3 * width, width), jnp.bfloat16),
            pltpu.VMEM(((levels + 2) * ROWS, width), jnp.float32),
            pltpu.VMEM(((levels + 2) * ROWS, width), jnp.float32),
            pltpu.VMEM((levels, width), jnp.float32),
            pltpu.VMEM((3, 16 * quads, width), jnp.float32),
            pltpu.VMEM((STEPS, 16 * quads, width), jnp.bfloat16),
            pltpu.VMEM((STEPS, 3, 16 * quads, width), jnp.bfloat16),
            pltpu.VMEM((tile_count, ROWS, width), jnp.float32),
            pltpu.VMEM((tile_count, ROWS, width), jnp.float32),
            pltpu.SemaphoreType.DMA((chunks,)),
            pltpu.SemaphoreType.DMA,
            pltpu.SemaphoreType.DMA((chunks,)),
            pltpu.SemaphoreType.DMA((STEPS, 2, 3)),
            pltpu.SemaphoreType.DMA((STEPS, 2, 3)),
            pltpu.SemaphoreType.DMA((tile_count,)),
            pltpu.SemaphoreType.DMA((tile_count,)),
        ],
        compiler_params=pltpu.CompilerParams(
            collective_id=0, has_side_effects=True, vmem_limit_bytes=40 << 20
        ),
    )(
        *(
            pltpu.with_memory_space_constraint(value, pltpu.HBM)
            for value in (
        tracer_state.transpose(1, 0, 2),
        krylov_direction.transpose(1, 0, 2),
        explicit_columns.T,
        wet_levels.reshape(1, width),
        surface_light.reshape(1, width),
        martin_exponent.reshape(1, width),
        column_slots,
        explicit_tiles.reshape(levels, -1, width),
        implicit_tiles.reshape(levels, -1, width),
            )
        )
    )
    return (state.transpose(1, 0, 2), tangent.transpose(1, 0, 2), flux.reshape(-1))


def solution(mesh):
    return jax.shard_map(
        on_device,
        mesh=mesh,
        in_specs=(
            P(None, None, ("groups", "tile")),
            P(None, None, ("groups", "tile")),
            P("tile", None, None, None),
            P("tile", None, None, None),
            P("tile", None),
            P("tile", None),
            P("tile"),
            P(("groups", "tile")),
            P(("groups", "tile")),
            P("tile", None),
        ),
        out_specs=(
            P(None, None, ("groups", "tile")),
            P(None, None, ("groups", "tile")),
            P(("groups", "tile")),
        ),
        check_vma=False,
    )
```

```python
import jax
import jax.numpy as jnp
from jax import lax
from jax.experimental import pallas as pl
from jax.experimental.pallas import tpu as pltpu
from jax.sharding import PartitionSpec as P

EUPHOTIC = 6
STEPS = 3

max_uptake = 1.0
half_saturation = 0.5
dop_fraction = 0.67
dop_decay = 0.2
time_step = 0.5

MESH = pl.DeviceIdType.MESH
ROWS = 8


def divisor(count, most):
    return max(n for n in range(1, most + 1) if count % n == 0)


def kernel(
    state_hbm,
    direction_hbm,
    columns_hbm,
    wet_hbm,
    light_hbm,
    martin_hbm,
    slots_hbm,
    explicit_hbm,
    implicit_hbm,
    state_out,
    tangent_out,
    flux_out,
    state_ref,
    direction_ref,
    columns_ref,
    wet_ref,
    light_ref,
    martin_ref,
    slots_ref,
    small_sem,
    local_tiles,
    ghost_tiles,
    implicit_tiles,
    fields,
    middle,
    remineral,
    ghost_mask,
    sending,
    arriving,
    flux_sending,
    flux_arriving,
    local_sem,
    ghost_tile_sem,
    implicit_sem,
    send_sem,
    recv_sem,
    flux_send_sem,
    flux_recv_sem,
):
    tile_count = lax.axis_size("tile")
    me = lax.axis_index("tile")
    levels, tracers, width = state_hbm.shape
    slot_count = slots_ref.shape[1]
    chunk = divisor(levels, 10)
    chunks = levels // chunk
    quads = sending.shape[1] // 16
    depth = 3 * width

    def peer_at(offset):
        return lax.rem(me + offset + tile_count, tile_count)

    local_copies = [
        pltpu.make_async_copy(
            explicit_hbm.at[pl.ds(c * chunk, chunk), pl.ds(0, depth), :],
            local_tiles.at[pl.ds(c * chunk, chunk)],
            local_sem.at[c],
        )
        for c in range(chunks)
    ]
    ghost_copy = pltpu.make_async_copy(
        explicit_hbm.at[pl.ds(0, 4 * quads), pl.ds(depth, depth), :],
        ghost_tiles,
        ghost_tile_sem,
    )
    implicit_copies = [
        pltpu.make_async_copy(
            implicit_hbm.at[pl.ds(c * chunk, chunk)],
            implicit_tiles.at[pl.ds(c * chunk, chunk)],
            implicit_sem.at[c],
        )
        for c in range(chunks)
    ]
    small_copies = [
        pltpu.make_async_copy(source, target, small_sem.at[i])
        for i, (source, target) in enumerate(
            (
                (state_hbm, state_ref),
                (direction_hbm, direction_ref),
                (wet_hbm, wet_ref),
                (light_hbm, light_ref),
                (martin_hbm, martin_ref),
                (columns_hbm, columns_ref),
                (slots_hbm, slots_ref),
            )
        )
    ]
    for copy in small_copies + local_copies + [ghost_copy] + implicit_copies:
        copy.start()

    barrier = pltpu.get_barrier_semaphore()
    for offset in range(1, tile_count):
        pl.semaphore_signal(
            barrier, inc=1, device_id={"tile": peer_at(offset)}, device_id_type=MESH
        )

    fields[...] = jnp.zeros_like(fields)
    flux_sending[...] = jnp.zeros_like(flux_sending)
    for copy in small_copies:
        copy.wait()
    for l in range(levels):
        fields[pl.ds((l + 1) * ROWS, tracers), :] = state_ref[l]
        fields[pl.ds((l + 1) * ROWS + tracers, tracers), :] = direction_ref[l]

    row = lax.broadcasted_iota(jnp.int32, (ROWS, width), 0)
    quad_row = lax.broadcasted_iota(jnp.int32, (2 * ROWS, width), 0) // 4
    upper = row < 4
    pieces = ((0, quads // 2), (quads // 2, quads))
    ghost_copies = [[] for _ in range(STEPS)]

    def at_level(l):
        return pl.ds(pl.multiple_of((l + 1) * ROWS, ROWS), ROWS)

    def pack_piece(step, piece):
        for q in range(*pieces[piece]):
            parts = [fields[at_level(4 * q + j), :] for j in range(4)]
            pairs = [
                jnp.where(upper, parts[2 * h], pltpu.roll(parts[2 * h + 1], 4, 0))
                for h in range(2)
            ]
            sending[step, pl.ds(16 * q, 16), :] = jnp.concatenate(pairs, 0).astype(
                jnp.bfloat16
            )

    def start_piece(step, piece):
        first, last = pieces[piece]
        rows = pl.ds(16 * first, 16 * (last - first))
        copies = [
            pltpu.make_async_remote_copy(
                src_ref=sending.at[step, rows],
                dst_ref=arriving.at[step, k, rows],
                send_sem=send_sem.at[step, piece, k],
                recv_sem=recv_sem.at[step, piece, k],
                device_id={"tile": peer_at(offset)},
                device_id_type=MESH,
            )
            for k, offset in ((2, tile_count // 2), (0, 1), (1, -1))
        ]
        for copy in copies:
            copy.start()
        ghost_copies[step].append(copies)

    def send_piece(step, piece):
        pack_piece(step, piece)
        start_piece(step, piece)

    for piece in range(2):
        pack_piece(0, piece)
    pl.semaphore_wait(barrier, tile_count - 1)
    for piece in range(2):
        start_piece(0, piece)

    depth_count = wet_ref[...].astype(jnp.float32)
    wet_limit = jnp.where(upper, jnp.broadcast_to(depth_count, (ROWS, width)), 0.0)
    light = light_ref[...]
    martin = martin_ref[...]

    zeros = jnp.zeros((ROWS, width), jnp.float32)
    middle[pl.ds(0, ROWS), :] = zeros
    middle[pl.ds((levels + 1) * ROWS, ROWS), :] = zeros

    level = lax.broadcasted_iota(jnp.int32, (levels, width), 0).astype(jnp.float32)

    def passing(at):
        ratio = jnp.log(jnp.maximum(at + 1.0, 1.0) / EUPHOTIC)
        reaching = jnp.where(at >= EUPHOTIC - 1, jnp.exp(-1.5 * martin * ratio), 1.0)
        kept = jnp.where(at < depth_count - 1.0, reaching, 0.0)
        return jnp.where(at < 0.0, 1.0, kept)

    remineral[...] = time_step * (passing(level - 1.0) - passing(level))

    for k in range(3):
        for l in range(4 * quads):
            shared = (columns_ref[3 + k : 4 + k, l : l + 1] != levels).astype(jnp.float32)
            ghost_mask[k, pl.ds(4 * l, 4), :] = jnp.broadcast_to(shared, (4, width))

    even = jnp.where((row == 0) | (row == 2), time_step * dop_decay, 0.0)
    odd = jnp.where((row == 1) | (row == 3), time_step * dop_decay, 0.0)
    lit = lax.broadcasted_iota(jnp.int32, (ROWS, width), 0).astype(jnp.float32)
    strength = jnp.where(
        (lit < EUPHOTIC) & (lit < depth_count),
        max_uptake * light * jnp.exp(-2.0 * lit / EUPHOTIC),
        0.0,
    )
    uptake_share = time_step * jnp.where(
        even > 0.0, -1.0, jnp.where(odd > 0.0, dop_fraction, 0.0)
    )

    def pair_product(first, second, tiles, l):
        blocks = [jnp.concatenate([part, zeros], 0) for part in first]
        blocks += [jnp.concatenate([zeros, part], 0) for part in second]
        return jnp.dot(
            jnp.concatenate(blocks, 1).astype(jnp.bfloat16),
            tiles[pl.ds(l, 2)].reshape(2 * depth, width),
            preferred_element_type=jnp.float32,
        )

    total = jnp.zeros((1, width), jnp.float32)
    flux_copies = []
    for step in range(STEPS):
        phosphate = fields[pl.ds(ROWS, ROWS, stride=ROWS), :]
        direction = fields[pl.ds(ROWS + tracers, ROWS, stride=ROWS), :]
        inverse = 1.0 / (half_saturation**2 + phosphate * phosphate)
        uptake = strength * (phosphate * phosphate) * inverse
        uptake_slope = (
            strength
            * (2.0 * half_saturation**2 * phosphate * inverse)
            * (direction * inverse)
        )
        export = (1.0 - dop_fraction) * jnp.sum(uptake, 0, keepdims=True)
        export_slope = (1.0 - dop_fraction) * jnp.sum(uptake_slope, 0, keepdims=True)
        total = total + export
        sinking = jnp.where(row == 0, export, jnp.where(row == 2, export_slope, 0.0))

        if step == STEPS - 1:
            by_column = jnp.transpose(jnp.broadcast_to(total, (width, width)))
            by_column = by_column[:, :slot_count]
            column = lax.broadcasted_iota(jnp.int32, (width, slot_count), 0)

            def fill(b, carry):
                picked = jnp.where(column == slots_ref[pl.ds(b, 1), :], by_column, 0.0)
                flux_sending[b, 0:1, 0:slot_count] = jnp.sum(picked, 0, keepdims=True)
                return carry

            lax.fori_loop(0, tile_count, fill, 0, unroll=2)
            for offset in range(1, tile_count):
                flux_copies.append(
                    pltpu.make_async_remote_copy(
                        src_ref=flux_sending.at[peer_at(offset)],
                        dst_ref=flux_arriving.at[me],
                        send_sem=flux_send_sem.at[offset],
                        recv_sem=flux_recv_sem.at[offset],
                        device_id={"tile": peer_at(offset)},
                        device_id_type=MESH,
                    )
                )
            for copy in flux_copies:
                copy.start()

        def explicit_chunk(c, carry):
            for i in range(chunk // 2):
                l = c * chunk + 2 * i
                near = [fields[at_level(l + n), :] for n in range(-1, 3)]
                first, second = (near[1], near[0], near[2]), (near[2], near[1], near[3])
                carried = pair_product(first, second, local_tiles, l)
                for n in range(2):
                    here = near[1 + n]
                    decay = even * pltpu.roll(here, ROWS - 1, 0) - odd * here
                    wet = (l + n).astype(jnp.float32) < wet_limit
                    middle[at_level(l + n), :] = (
                        carried[n * ROWS : (n + 1) * ROWS]
                        + jnp.where(wet, decay, 0.0)
                        + remineral[pl.ds(l + n, 1), :] * sinking
                    )
            return carry

        if step == 0:
            for c in range(chunks):
                local_copies[c].wait()
                lax.fori_loop(c, c + 1, explicit_chunk, 0)
        else:
            lax.fori_loop(0, chunks, explicit_chunk, 0)

        for l in range(EUPHOTIC):
            share = jnp.where(
                row < 2, uptake[l : l + 1, :], uptake_slope[l : l + 1, :]
            )
            middle[at_level(l), :] = middle[at_level(l), :] + uptake_share * share

        def ghost_quad(q, carry):
            rows = pl.ds(pl.multiple_of(16 * q, 16), 16)
            sources = [
                arriving[step, k, rows, :].astype(jnp.float32) * ghost_mask[k, rows, :]
                for k in range(3)
            ]
            blocks = [
                jnp.where(quad_row == j, sources[k], 0.0)
                for j in range(4)
                for k in range(3)
            ]
            carried = jnp.dot(
                jnp.concatenate(blocks, 1).astype(jnp.bfloat16),
                ghost_tiles[pl.ds(4 * q, 4)].reshape(4 * depth, width),
                preferred_element_type=jnp.float32,
            )
            for j in range(4):
                part = carried[ROWS * (j // 2) : ROWS * (j // 2) + ROWS]
                if j % 2:
                    part = pltpu.roll(part, 4, 0)
                l = 4 * q + j
                middle[at_level(l), :] = middle[at_level(l), :] + jnp.where(
                    upper, part, 0.0
                )
            return carry

        def implicit_pairs(p, carry):
            l = 2 * p
            near = [middle[at_level(l + n), :] for n in range(-1, 3)]
            settled = pair_product(near[:3], near[1:], implicit_tiles, l)
            for n in range(2):
                wet = (l + n).astype(jnp.float32) < wet_limit
                fields[at_level(l + n), :] = jnp.where(
                    wet, settled[n * ROWS : (n + 1) * ROWS], 0.0
                )
            return carry

        def settle(low, high):
            while step == 0 and len(loaded) * chunk < high:
                implicit_copies[len(loaded)].wait()
                loaded.append(high)
            pairs = (high - low) // 2
            lax.fori_loop(
                low // 2, high // 2, implicit_pairs, 0, unroll=divisor(pairs, 12)
            )

        loaded = []
        split = 4 * pieces[0][1]
        deep = 4 * quads + 2
        if step == STEPS - 1:
            settle(deep, levels)
        if step == 0:
            ghost_copy.wait()
        for piece, (first, last) in enumerate(pieces):
            for copy in ghost_copies[step][piece]:
                copy.wait_recv()
            lax.fori_loop(first, last, ghost_quad, 0, unroll=2)
            if piece == 0:
                settle(0, split - 2)
        if step == STEPS - 1:
            settle(split - 2, deep)
        else:
            settle(split - 2, split)
            send_piece(step + 1, 0)
            settle(split, 4 * quads)
            send_piece(step + 1, 1)
            settle(4 * quads, levels)
        for copies in ghost_copies[step]:
            for copy in copies:
                copy.wait_send()

    for l in range(levels):
        state_out[l] = fields[pl.ds((l + 1) * ROWS, tracers), :]
        tangent_out[l] = fields[pl.ds((l + 1) * ROWS + tracers, tracers), :]
    for copy in flux_copies:
        copy.wait()
    flux_arriving[me] = flux_sending[me]
    for s in range(tile_count):
        flux_out[s : s + 1, :] = flux_arriving[s, 0:1, 0:slot_count]


def on_device(
    tracer_state,
    krylov_direction,
    explicit_tiles,
    implicit_tiles,
    explicit_columns,
    ghost_levels,
    wet_levels,
    surface_light,
    martin_exponent,
    column_slots,
):
    tracers, levels, width = tracer_state.shape
    tile_count = lax.axis_size("tile")
    slot_count = column_slots.shape[1]
    quads = -(-ghost_levels.shape[1] // 4)
    chunks = levels // divisor(levels, 10)
    vmem = pl.BlockSpec(memory_space=pltpu.VMEM)
    hbm = pl.BlockSpec(memory_space=pltpu.HBM)
    state, tangent, flux = pl.pallas_call(
        kernel,
        out_shape=(
            jax.ShapeDtypeStruct((levels, tracers, width), jnp.float32),
            jax.ShapeDtypeStruct((levels, tracers, width), jnp.float32),
            jax.ShapeDtypeStruct((tile_count, slot_count), jnp.float32),
        ),
        in_specs=[hbm] * 9,
        out_specs=(vmem, vmem, vmem),
        scratch_shapes=[
            pltpu.VMEM((levels, tracers, width), jnp.float32),
            pltpu.VMEM((levels, tracers, width), jnp.float32),
            pltpu.VMEM(explicit_columns.shape[::-1], jnp.int32),
            pltpu.VMEM((1, width), jnp.int32),
            pltpu.VMEM((1, width), jnp.float32),
            pltpu.VMEM((1, width), jnp.float32),
            pltpu.VMEM(column_slots.shape, jnp.int32),
            pltpu.SemaphoreType.DMA((7,)),
            pltpu.VMEM((levels, 3 * width, width), jnp.bfloat16),
            pltpu.VMEM((4 * quads, 3 * width, width), jnp.bfloat16),
            pltpu.VMEM((levels, 3 * width, width), jnp.bfloat16),
            pltpu.VMEM(((levels + 2) * ROWS, width), jnp.float32),
            pltpu.VMEM(((levels + 2) * ROWS, width), jnp.float32),
            pltpu.VMEM((levels, width), jnp.float32),
            pltpu.VMEM((3, 16 * quads, width), jnp.float32),
            pltpu.VMEM((STEPS, 16 * quads, width), jnp.bfloat16),
            pltpu.VMEM((STEPS, 3, 16 * quads, width), jnp.bfloat16),
            pltpu.VMEM((tile_count, ROWS, width), jnp.float32),
            pltpu.VMEM((tile_count, ROWS, width), jnp.float32),
            pltpu.SemaphoreType.DMA((chunks,)),
            pltpu.SemaphoreType.DMA,
            pltpu.SemaphoreType.DMA((chunks,)),
            pltpu.SemaphoreType.DMA((STEPS, 2, 3)),
            pltpu.SemaphoreType.DMA((STEPS, 2, 3)),
            pltpu.SemaphoreType.DMA((tile_count,)),
            pltpu.SemaphoreType.DMA((tile_count,)),
        ],
        compiler_params=pltpu.CompilerParams(
            collective_id=0, has_side_effects=True, vmem_limit_bytes=40 << 20
        ),
    )(
        *(
            pltpu.with_memory_space_constraint(value, pltpu.HBM)
            for value in (
        tracer_state.transpose(1, 0, 2),
        krylov_direction.transpose(1, 0, 2),
        explicit_columns.T,
        wet_levels.reshape(1, width),
        surface_light.reshape(1, width),
        martin_exponent.reshape(1, width),
        column_slots,
        explicit_tiles.reshape(levels, -1, width),
        implicit_tiles.reshape(levels, -1, width),
            )
        )
    )
    return (state.transpose(1, 0, 2), tangent.transpose(1, 0, 2), flux.reshape(-1))


def solution(mesh):
    return jax.shard_map(
        on_device,
        mesh=mesh,
        in_specs=(
            P(None, None, ("groups", "tile")),
            P(None, None, ("groups", "tile")),
            P("tile", None, None, None),
            P("tile", None, None, None),
            P("tile", None),
            P("tile", None),
            P("tile"),
            P(("groups", "tile")),
            P(("groups", "tile")),
            P("tile", None),
        ),
        out_specs=(
            P(None, None, ("groups", "tile")),
            P(None, None, ("groups", "tile")),
            P(("groups", "tile")),
        ),
        check_vma=False,
    )
```
